256 devices in a mesh: ctx: 32 (over x, y, core), head: 8 (over z).
Axes of the slice: x: 4, y: 4, z: 8, core: 2. Of those that a mesh axis runs over, the one named last changes fastest.
Arguments:
- features: bfloat16 [16384, 8192], P('ctx', 'head'), may hold values from -6 to 6
- gate_values: bfloat16 [16384, 8192], P('ctx', 'head'), may hold values from -6 to 6
- write_proj: bfloat16 [16384, 1024], P('ctx', 'head'), may hold values from -0.0234375 to 0.0234375
- read_proj: bfloat16 [16384, 1024], P('ctx', 'head'), may hold values from -6 to 6
- step_size: float32 [128, 16384], P('head', 'ctx'), may hold values from 0.25 to 2
- log_decay: float32 [128, 16384], P('head', 'ctx'), may hold values from -1 to 0
- starts: int32 [16384], P('ctx'), may hold values from 0 to 1
- skip_weight: float32 [128], P('head'), may hold values from 0.5 to 1.5
- norm_gain: float32 [8192], P('head'), may hold values from 0.1 to 1.9
- out_weight: bfloat16 [8192, 4096], P('head'), may hold values from -0.0625 to 0.0625
Outputs:
- mixed: bfloat16 [16384, 4096], P(('ctx', 'head'))
The draws below stay inside these ranges and needn't reach their ends.
All inputs are finite; a program needn't handle non-finite values.
Results may differ from the reference program's by a relative error of at most 0.0061.
Values sent between devices are 32-bit elements; how exact they have to be, the bound alone decides.
A program may use at most 128 MiB of HBM per device.

```python
import math
import jax
import jax.numpy as jnp
from jax import lax

D = 4096
HEADS = 128
HEAD_DIM = 64
NSTATE = 128
GROUPS = 8
SPAN = 256
TOK_DEV = 512
SEQUENCE_SPAN = 16384
INNER = 8192


def draw_log_decay(key, part):
    floor_offset = jax.random.fold_in(key, 7)
    seed_selection, seed_gradual, seed_quick, seed_jagged, seed_spike, seed_extent = jax.random.split(floor_offset, 6)
    slow_rate = jnp.exp(jax.random.uniform(seed_gradual, (HEADS,), jnp.float32, math.log(0.05 / SEQUENCE_SPAN), math.log(0.5 / SEQUENCE_SPAN)))
    fast_rate = jnp.exp(jax.random.uniform(seed_quick, (HEADS,), jnp.float32, math.log(0.02), math.log(0.05)))
    picked = jax.random.randint(seed_selection, (HEADS,), 0, 2) == 0
    fading_rate = jnp.where(picked, fast_rate, slow_rate)
    jagged_perturbation = jnp.exp(jax.random.uniform(seed_jagged, (HEADS, SEQUENCE_SPAN), jnp.float32, -0.7, 0.7))
    spike_present = jax.random.randint(seed_spike, (SEQUENCE_SPAN,), 0, max(SEQUENCE_SPAN // 2, 1)) == 0
    spike_magnitude = jnp.where(spike_present, jax.random.uniform(seed_extent, (SEQUENCE_SPAN,), jnp.float32, 0.2, 0.5), 0.0)
    return -(fading_rate[:, None] * jagged_perturbation) - spike_magnitude[None, :]


def draw_starts(key, part):
    folded = jax.random.fold_in(key, 11)
    seed_which, seed_lottery, seed_planted = jax.random.split(folded, 3)
    quarter = SEQUENCE_SPAN // 4
    which_end = jax.random.randint(seed_which, (), 0, 2)
    region_first = which_end * (SEQUENCE_SPAN - quarter)
    position = jnp.arange(SEQUENCE_SPAN, dtype=jnp.int32)
    within_region = (position >= region_first) & (position < region_first + quarter)
    lottery = jax.random.randint(seed_lottery, (SEQUENCE_SPAN,), 0, TOK_DEV) == 0
    planted = region_first + jax.random.randint(seed_planted, (), 0, quarter)
    return jnp.where(within_region & lottery | (position == planted), 1, 0).astype(jnp.int32)


def level_of(own_key, dims, pieces, least, high):
    loudness = 1.0
    for dim, parts in pieces:
        steps = jax.random.uniform(jax.random.fold_in(jax.random.fold_in(own_key, 6), dim), (parts,), jnp.float32, least / len(pieces), high / len(pieces))
        loudness = loudness * jnp.repeat(jnp.exp(steps), dims[dim] // parts).reshape((-1,) + (1,) * (len(dims) - 1 - dim))
    return loudness


def normal_values(own_key, dims, scale, reach, cuts=(), kind=jnp.bfloat16):
    entries = scale * jax.random.normal(own_key, dims, jnp.float32)
    if cuts:
        entries = entries * level_of(own_key, dims, cuts, -0.22, 0.18)
    return jnp.clip(entries, -reach, reach).astype(kind)


def setup_inputs(seed: int = 0) -> dict:
    splits = jax.random.split(jax.random.key(seed), 11)
    features = normal_values(splits[0], (SEQUENCE_SPAN, INNER), 1.0, 6.0, ((0, 32), (1, 8)))
    gate_values = normal_values(splits[1], (SEQUENCE_SPAN, INNER), 1.0, 6.0, ((0, 32), (1, 8)))
    write_proj = normal_values(splits[2], (SEQUENCE_SPAN, GROUPS * NSTATE), (1.0 / (NSTATE * TOK_DEV) ** 0.5), 0.0234375, ((0, 32), (1, 8)))
    read_proj = normal_values(splits[3], (SEQUENCE_SPAN, GROUPS * NSTATE), 1.0, 6.0, ((0, 32), (1, 8)))
    step_size = jnp.clip(jnp.exp(math.log(2.0) - 2.0794415 * jax.random.uniform(splits[4], (HEADS, SEQUENCE_SPAN), jnp.float32) ** level_of(splits[4], (HEADS, SEQUENCE_SPAN), ((0, 8), (1, 32)), -0.2, 0.2)), 0.25, 2.0)
    log_decay = draw_log_decay(jax.random.fold_in(splits[10], 71), 0)
    starts = draw_starts(jax.random.fold_in(splits[10], 71), 0)
    skip_weight = jnp.clip(0.5 + 1.0 * jax.random.uniform(splits[7], (HEADS,), jnp.float32) ** level_of(splits[7], (HEADS,), ((0, 8),), -0.2, 0.2), 0.5, 1.5)
    norm_gain = jnp.clip(1.0 + 0.18 * jax.random.normal(splits[8], (INNER,), jnp.float32), 0.1, 1.9)
    out_weight = normal_values(splits[9], (INNER, D), INNER ** -0.5, 0.0625, ((0, 8),))
    return dict(features=features, gate_values=gate_values, write_proj=write_proj, read_proj=read_proj, step_size=step_size, log_decay=log_decay, starts=starts, skip_weight=skip_weight, norm_gain=norm_gain, out_weight=out_weight)


eps = 1e-05

def reference(features, gate_values, write_proj, read_proj, step_size, log_decay, starts, skip_weight, norm_gain, out_weight):
    blocks = SEQUENCE_SPAN // SPAN
    per_group = HEADS // GROUPS
    feat_all = features.reshape(blocks, SPAN, HEADS, HEAD_DIM)
    gate_all = gate_values.reshape(blocks, SPAN, INNER)
    write_all = write_proj.reshape(blocks, SPAN, GROUPS, NSTATE)
    read_all = read_proj.reshape(blocks, SPAN, GROUPS, NSTATE)
    step_all = step_size.reshape(HEADS, blocks, SPAN).transpose(1, 0, 2)
    decay_all = log_decay.reshape(HEADS, blocks, SPAN).transpose(1, 0, 2)
    start_all = starts.reshape(blocks, SPAN)
    position = jnp.arange(SPAN)
    causal = position[:, None] >= position[None, :]

    def advance(hidden_state, inputs):
        feat_blk, gate_blk, write_blk, read_blk, step_blk, decay_blk, start_blk = inputs
        running = jnp.cumsum(decay_blk, axis=1)
        seg_local = jnp.cumsum(start_blk)
        together = (seg_local[:, None] == seg_local[None, :]) & causal
        spread_log = running[:, :, None] - running[:, None, :]
        damping = jnp.where(together[None], jnp.exp(jnp.where(together[None], spread_log, 0.0)), 0.0)
        scores = jnp.einsum('ign,jgn->gij', read_blk.astype(jnp.float32), write_blk.astype(jnp.float32))
        weights = ((damping * step_blk[:, None, :]).reshape(GROUPS, per_group, SPAN, SPAN) * scores[:, None]).astype(jnp.bfloat16)
        weights = weights.reshape(HEADS, SPAN, SPAN)
        intra_out = jnp.einsum('hij,jhp->ihp', weights.astype(jnp.float32), feat_blk.astype(jnp.float32))
        entry_read = lax.optimization_barrier(hidden_state.astype(jnp.bfloat16)).astype(jnp.float32)
        carried_out = jnp.einsum('ign,gepn->igep', read_blk.astype(jnp.float32), entry_read.reshape(GROUPS, per_group, HEAD_DIM, NSTATE)).reshape(SPAN, HEADS, HEAD_DIM)
        reach_scale = jnp.where(seg_local[None, :] == 0, jnp.exp(running), 0.0).T
        mixed_out = intra_out + reach_scale[:, :, None] * carried_out + skip_weight[None, :, None] * feat_blk.astype(jnp.float32)
        gated = mixed_out.reshape(SPAN, INNER) * jax.nn.silu(gate_blk.astype(jnp.float32))
        grouped = gated.reshape(SPAN, GROUPS, INNER // GROUPS)
        mean_square = lax.optimization_barrier(jnp.mean(grouped * grouped, axis=-1, keepdims=True))
        normed = ((grouped * lax.rsqrt(mean_square + eps)).reshape(SPAN, INNER) * norm_gain[None, :]).astype(jnp.bfloat16)
        block_out = jnp.dot(normed, out_weight, preferred_element_type=jnp.float32).astype(jnp.bfloat16)
        tail_scale = jnp.where(seg_local[None, :] == seg_local[-1], jnp.exp(running[:, -1:] - running), 0.0) * step_blk
        scaled_in = (tail_scale.T[:, :, None] * feat_blk.astype(jnp.float32)).astype(jnp.bfloat16)
        block_state = jnp.einsum('jgep,jgn->gepn', scaled_in.astype(jnp.float32).reshape(SPAN, GROUPS, per_group, HEAD_DIM), write_blk.astype(jnp.float32)).reshape(HEADS, HEAD_DIM, NSTATE)
        keep_scale = jnp.where(seg_local[-1] == 0, jnp.exp(running[:, -1]), 0.0)
        hidden_state = keep_scale[:, None, None] * hidden_state + block_state
        return (hidden_state, block_out)
    initial = jnp.zeros((HEADS, HEAD_DIM, NSTATE), jnp.float32)
    final_state, outputs = lax.scan(advance, initial, (feat_all, gate_all, write_all, read_all, step_all, decay_all, start_all))
    return outputs.reshape(SEQUENCE_SPAN, D)
```

```python
import functools

import jax
import jax.numpy as jnp
from jax import lax
from jax.experimental import pallas as pl
from jax.experimental.pallas import tpu as pltpu
from jax.sharding import PartitionSpec as P

MESH = pl.DeviceIdType.MESH
F32 = jnp.float32
BF16 = jnp.bfloat16

HEAD_DIM = 64
NSTATE = 128
SPAN = 256
EPS = 1e-05
MASKED = -1e30
PIECES = 4
EARLY = (4, 4)


def split3(value):
    high = value.astype(BF16)
    rest = value - high.astype(F32)
    mid = rest.astype(BF16)
    low = (rest - mid.astype(F32)).astype(BF16)
    return high, mid, low


def kernel(
    n_ctx,
    n_head,
    feat_hbm,
    gate_hbm,
    write_hbm,
    read_hbm,
    step_hbm,
    decay_hbm,
    starts_hbm,
    skip_hbm,
    gain_hbm,
    weight_hbm,
    out_ref,
    feat,
    gate,
    write,
    read,
    step,
    decay,
    starts,
    skip,
    gain,
    weight,
    write_t,
    rows_u,
    rows_seg,
    cols,
    expand,
    skip_row,
    ready,
    reach,
    state0,
    keep0,
    total,
    partner_part,
    first_state,
    send1,
    recv1,
    send2,
    recv2,
    send3,
    recv3,
    entry,
    normed,
    ring,
    in_sem,
    pair_send,
    pair_recv,
    ex_send,
    ex_recv,
    ring_send,
    ring_recv,
):
    ctx = lax.axis_index("ctx")
    z = lax.axis_index("head")
    core = lax.rem(ctx, 2)
    chip = ctx // 2
    chips = n_ctx // 2
    other = ctx + 1 - 2 * core
    heads = step.shape[0]
    blocks, span, chans = feat.shape
    half = chans // 2
    chunk = blocks * span // n_head
    per_block = span // chunk
    width = ring.shape[3]
    target = lax.rem(z + 1 + (n_head - 2) * core, n_head)

    barrier = pltpu.get_barrier_semaphore()
    pl.semaphore_signal(barrier, inc=1, device_id={"ctx": other, "head": z}, device_id_type=MESH)
    for offset in (1, n_head - 1):
        pl.semaphore_signal(
            barrier, inc=1, device_id={"ctx": ctx, "head": lax.rem(z + offset, n_head)}, device_id_type=MESH
        )

    def greet(offset, carry):
        peer = 2 * lax.rem(chip + offset, chips) + core
        pl.semaphore_signal(barrier, inc=1, device_id={"ctx": peer, "head": z}, device_id_type=MESH)
        return carry

    lax.fori_loop(1, chips, greet, 0)

    loads = {}
    for index, (name, source, dest) in enumerate(
        [
            ("decay", decay_hbm, decay),
            ("starts", starts_hbm, starts),
            ("step", step_hbm, step),
            ("write", write_hbm, write),
            ("feat", feat_hbm, feat),
            ("read", read_hbm, read),
            ("gate", gate_hbm, gate),
            ("skip", skip_hbm, skip),
            ("gain", gain_hbm, gain),
            ("weight", weight_hbm, weight),
        ]
    ):
        loads[name] = pltpu.make_async_copy(source, dest, in_sem.at[index])
        loads[name].start()

    row_id = lax.broadcasted_iota(jnp.int32, (span, span), 0)
    col_id = lax.broadcasted_iota(jnp.int32, (span, span), 1)
    upto = (row_id <= col_id).astype(F32).astype(BF16)
    head_of = lax.broadcasted_iota(jnp.int32, (heads, chans), 1) // HEAD_DIM
    pick = (head_of == lax.broadcasted_iota(jnp.int32, (heads, chans), 0)).astype(F32)

    def spread(column):
        return jnp.sum(column * pick, axis=0, keepdims=True)

    lane_head = lax.broadcasted_iota(jnp.int32, (1, 256), 1) // HEAD_DIM

    def diagonal(stacked, rows):
        result = stacked[0:rows]
        for i in range(1, 4):
            result = jnp.where(lane_head == i, stacked[i * rows : (i + 1) * rows], result)
        return result

    loads["decay"].wait()
    loads["starts"].wait()
    sums = []
    for k in range(blocks):
        tokens = slice(k * span, (k + 1) * span)
        start_rows = jnp.broadcast_to(starts[:, tokens].astype(F32), (heads, span)).astype(BF16)
        stacked = jnp.concatenate([*split3(decay[:, tokens]), start_rows], axis=0)
        sums.append(jnp.dot(stacked, upto, preferred_element_type=F32))
    loads["step"].wait()
    loads["write"].wait()
    keeps, states, tails, cums, segs = [], [], [], [], []
    for k in range(blocks):
        tokens = slice(k * span, (k + 1) * span)
        cum = sums[k][0:heads] + sums[k][heads : 2 * heads] + sums[k][2 * heads : 3 * heads]
        seg = sums[k][3 * heads : 3 * heads + 1]
        last = cum[:, span - 1 : span]
        seg_last = seg[:, span - 1 : span]
        tails.append(jnp.where(seg == seg_last, jnp.exp(last - cum), 0.0) * step[:, tokens])
        keeps.append(spread(jnp.where(seg_last == 0.0, jnp.exp(last), 0.0)))
        cums.append(cum)
        segs.append(seg)
    loads["feat"].wait()
    for k in range(blocks):
        turned = jnp.transpose(write[k].astype(F32))
        write_t[k] = turned.astype(BF16)
        parts = []
        for quad in range(heads // 4):
            lhs = jnp.concatenate(
                [(turned * tails[k][4 * quad + i : 4 * quad + i + 1]).astype(BF16) for i in range(4)], axis=0
            )
            full = jnp.dot(lhs, feat[k, :, 256 * quad : 256 * (quad + 1)], preferred_element_type=F32)
            parts.append(diagonal(full, NSTATE))
        states.append(parts)
    per_half = half // 256
    for h in range(2):
        cut = slice(h * half, (h + 1) * half)
        keep0[h] = jnp.broadcast_to(keeps[0][:, cut], (8, half))
        total[h, NSTATE:] = jnp.broadcast_to((keeps[0] * keeps[1])[:, cut], (8, half))
        for part in range(per_half):
            lanes = slice(256 * part, 256 * (part + 1))
            chans_at = slice(h * half + 256 * part, h * half + 256 * (part + 1))
            first = states[0][h * per_half + part]
            state0[h, :, lanes] = first
            total[h, :NSTATE, lanes] = keeps[1][:, chans_at] * first + states[1][h * per_half + part]

    pl.semaphore_wait(barrier, chips + 2)
    pair1 = pltpu.make_async_remote_copy(
        src_ref=total.at[1 - core],
        dst_ref=partner_part,
        send_sem=pair_send.at[0],
        recv_sem=pair_recv.at[0],
        device_id={"ctx": other, "head": z},
        device_id_type=MESH,
    )
    pair1.start()

    def columns_of_block(k):
        tokens = slice(k * span, (k + 1) * span)
        rows_u[k] = cums[k] - jnp.log(step[:, tokens])
        rows_seg[k] = jnp.broadcast_to(segs[k], (8, span))
        reach_scale = jnp.where(segs[k] == 0.0, jnp.exp(cums[k]), 0.0)
        pieces = [part.astype(F32) for part in split3(reach_scale)]
        seg_rows = jnp.broadcast_to(segs[k], (heads, span))
        pad = jnp.zeros((NSTATE - 5 * heads, span), F32)
        cols[tokens] = jnp.transpose(jnp.concatenate([cums[k], *pieces, seg_rows, pad], axis=0))

    for k in range(blocks):
        columns_of_block(k)
    line = lax.broadcasted_iota(jnp.int32, (NSTATE, chans), 0)
    owner = lax.broadcasted_iota(jnp.int32, (NSTATE, chans), 1) // HEAD_DIM
    inside = (line >= heads) & (line < 4 * heads)
    expand[...] = jnp.where(inside & (lax.rem(line, heads) == owner), 1.0, 0.0).astype(BF16)
    loads["skip"].wait()
    square = jnp.broadcast_to(skip[...], (heads, heads))
    same = lax.broadcasted_iota(jnp.int32, (heads, heads), 0) == lax.broadcasted_iota(jnp.int32, (heads, heads), 1)
    skip_row[...] = spread(jnp.sum(jnp.where(same, square, 0.0), axis=1, keepdims=True))
    ring[0] = jnp.zeros_like(ring[0])

    pair1.wait_recv()
    mine = total[core]
    theirs = partner_part[...]
    leads = core == 0
    s0 = jnp.where(leads, mine[:NSTATE], theirs[:NSTATE])
    s1 = jnp.where(leads, theirs[:NSTATE], mine[:NSTATE])
    m0 = jnp.where(leads, mine[NSTATE:], theirs[NSTATE:])
    m1 = jnp.where(leads, theirs[NSTATE:], mine[NSTATE:])
    first_state[:NSTATE] = s0
    first_state[NSTATE:] = m0
    joined = m1[0:1] * s0 + s1
    joined_mult = m0 * m1
    across = half // 128
    deep = NSTATE // (chips // across)
    for q in range(chips):
        rows = slice(deep * (q // across), deep * (q // across + 1))
        lanes = slice(128 * (q % across), 128 * (q % across + 1))
        send1[q, :deep] = joined[rows, lanes]
        send1[q, deep:] = joined_mult[:, lanes]

    def exchange1(offset):
        peer = lax.rem(chip + offset, chips)
        return pltpu.make_async_remote_copy(
            src_ref=send1.at[peer],
            dst_ref=recv1.at[chip],
            send_sem=ex_send.at[0, peer],
            recv_sem=ex_recv.at[0, chip],
            device_id={"ctx": 2 * peer + core, "head": z},
            device_id_type=MESH,
        )

    def start1(offset, carry):
        exchange1(offset).start()
        return carry

    lax.fori_loop(1, chips, start1, 0)
    recv1[chip] = send1[chip]

    def chunk_of(s):
        return lax.rem(z + (1 - core) * (n_head - 1 - s) + core * (1 + s), n_head)

    loads["read"].wait()
    loads["gate"].wait()
    loads["gain"].wait()

    def prepare(s):
        b = chunk_of(s)
        k = b // per_block
        local = pl.multiple_of(lax.rem(b, per_block) * chunk, chunk)
        at = pl.multiple_of(b * chunk, chunk)
        scores = jnp.dot(read[k, pl.ds(local, chunk), :], write_t[k], preferred_element_type=F32)
        column = cols[pl.ds(at, chunk), :]
        seg_row = rows_seg[k][0:1]
        seg_col = column[:, 4 * heads : 4 * heads + 1]
        later = local + lax.broadcasted_iota(jnp.int32, (chunk, span), 0)
        earlier = lax.broadcasted_iota(jnp.int32, (chunk, span), 1)
        mask = jnp.where((seg_col == seg_row) & (earlier <= later), 0.0, MASKED)
        u = rows_u[k]
        scale = jnp.dot(column.astype(BF16), expand[...], preferred_element_type=F32)
        for quad in range(heads // 4):
            lanes = slice(256 * quad, 256 * (quad + 1))
            stack = []
            for h in range(4 * quad, 4 * quad + 4):
                spread_log = column[:, h : h + 1] - u[h : h + 1] + mask
                stack.append((jnp.exp(spread_log) * scores).astype(BF16))
            full = jnp.dot(jnp.concatenate(stack, axis=0), feat[k, :, lanes], preferred_element_type=F32)
            gates = gate[k, pl.ds(local, chunk), lanes].astype(F32)
            silu = gates * jax.nn.sigmoid(gates)
            direct = skip_row[:, lanes] * feat[k, pl.ds(local, chunk), lanes].astype(F32)
            ready[s, :, lanes] = (diagonal(full, chunk) + direct) * silu
            reach[s, :, lanes] = scale[:, lanes] * silu

    def prepare_loop(low, high):
        def run(s, carry):
            prepare(s)
            return carry

        lax.fori_loop(low, high, run, 0)

    prepare_loop(0, EARLY[0])

    def back(peer):
        return pltpu.make_async_remote_copy(
            src_ref=send2.at[peer],
            dst_ref=recv2.at[chip],
            send_sem=ex_send.at[1, peer],
            recv_sem=ex_recv.at[1, chip],
            device_id={"ctx": 2 * peer + core, "head": z},
            device_id_type=MESH,
        )

    def arrival(round_, peer, dest):
        return pltpu.make_async_remote_copy(
            src_ref=dest.at[peer],
            dst_ref=dest.at[peer],
            send_sem=ex_send.at[round_, peer],
            recv_sem=ex_recv.at[round_, peer],
            device_id={"ctx": 2 * peer + core, "head": z},
            device_id_type=MESH,
        )

    def scan_step(p, state):
        send2[p] = state

        @pl.when(p != chip)
        def _():
            back(p).start()
            arrival(0, p, recv1).wait_recv()

        return recv1[p, deep : deep + 1] * state + recv1[p, :deep]

    lax.fori_loop(0, chips, scan_step, jnp.zeros((deep, 128), F32))
    recv2[chip] = send2[chip]

    prepare_loop(EARLY[0], EARLY[0] + EARLY[1])

    def await2(offset, carry):
        arrival(1, lax.rem(chip + offset, chips), recv2).wait_recv()
        return carry

    lax.fori_loop(1, chips, await2, 0)
    strips = []
    for down in range(chips // across):
        strips.append(jnp.concatenate([recv2[down * across + right] for right in range(across)], axis=1))
    entry0 = jnp.concatenate(strips, axis=0)
    entry1 = first_state[NSTATE : NSTATE + 1] * entry0 + first_state[:NSTATE]
    send3[...] = jnp.where(leads, entry1, entry0)
    pair2 = pltpu.make_async_remote_copy(
        src_ref=send3,
        dst_ref=recv3,
        send_sem=pair_send.at[1],
        recv_sem=pair_recv.at[1],
        device_id={"ctx": other, "head": z},
        device_id_type=MESH,
    )
    pair2.start()

    def set_entry(h, value):
        entry[0, h] = value.astype(BF16)
        entry[1, h] = (keep0[h][0:1] * value + state0[h]).astype(BF16)

    set_entry(core, jnp.where(leads, entry0, entry1))
    loads["weight"].wait()
    pair2.wait_recv()
    set_entry(1 - core, recv3[...])

    def hop(s, piece):
        return pltpu.make_async_remote_copy(
            src_ref=ring.at[s, piece],
            dst_ref=ring.at[s + 1, piece],
            send_sem=ring_send.at[s, piece],
            recv_sem=ring_recv.at[s, piece],
            device_id={"ctx": ctx, "head": target},
            device_id_type=MESH,
        )

    def ring_step(s, carry):
        b = chunk_of(s)
        k = b // per_block
        local = pl.multiple_of(lax.rem(b, per_block) * chunk, chunk)
        reads = read[k, pl.ds(local, chunk), :]
        gated = []
        squares = jnp.zeros((chunk, 1), F32)
        for h in range(2):
            lanes = slice(h * half, (h + 1) * half)
            carried = jnp.dot(reads, entry[k, h], preferred_element_type=F32)
            value = ready[s, :, lanes] + reach[s, :, lanes] * carried
            squares = squares + jnp.sum(value * value, axis=1, keepdims=True)
            gated.append(value)
        scale = lax.rsqrt(squares * (1.0 / chans) + EPS)
        for h in range(2):
            lanes = slice(h * half, (h + 1) * half)
            normed[:, lanes] = (gated[h] * scale * gain[:, lanes]).astype(BF16)
        for piece in range(PIECES):
            lanes = slice(piece * width, (piece + 1) * width)
            own = jnp.dot(normed[...], weight[:, lanes], preferred_element_type=F32)

            @pl.when(s > 0)
            def _():
                hop(s - 1, piece).wait_recv()

            ring[s, piece] = ring[s, piece] + own

            @pl.when(s < n_head - 1)
            def _():
                hop(s, piece).start()


        return carry

    lax.fori_loop(0, n_head, ring_step, 0)
    for piece in range(PIECES):
        out_ref[:, piece * width : (piece + 1) * width] = ring[n_head - 1, piece].astype(BF16)

    pair1.wait_send()
    pair2.wait_send()

    def drain(offset, carry):
        peer = lax.rem(chip + offset, chips)
        arrival(0, peer, recv1).wait_send()
        arrival(1, peer, recv2).wait_send()
        return carry

    lax.fori_loop(1, chips, drain, 0)

    def drain_ring(s, carry):
        for piece in range(PIECES):
            hop(s, piece).wait_send()
        return carry

    lax.fori_loop(0, n_head - 1, drain_ring, 0)


def solution(mesh):
    n_ctx, n_head = mesh.shape["ctx"], mesh.shape["head"]

    def body(features, gate_values, write_proj, read_proj, step_size, log_decay, starts, skip_weight, norm_gain, out_weight):
        tokens, chans = features.shape
        heads = step_size.shape[0]
        blocks = tokens // SPAN
        width_out = out_weight.shape[1]
        chunk = tokens // n_head
        half = chans // 2
        chips = n_ctx // 2
        across = half // 128
        deep = NSTATE // (chips // across)
        width = width_out // PIECES
        dma = pltpu.SemaphoreType.DMA
        scratch = [
            pltpu.VMEM((blocks, SPAN, chans), BF16),
            pltpu.VMEM((blocks, SPAN, chans), BF16),
            pltpu.VMEM((blocks, SPAN, NSTATE), BF16),
            pltpu.VMEM((blocks, SPAN, NSTATE), BF16),
            pltpu.VMEM((heads, tokens), F32),
            pltpu.VMEM((heads, tokens), F32),
            pltpu.VMEM((1, tokens), jnp.int32),
            pltpu.VMEM((1, heads), F32),
            pltpu.VMEM((1, chans), F32),
            pltpu.VMEM((chans, width_out), BF16),
            pltpu.VMEM((blocks, NSTATE, SPAN), BF16),
            pltpu.VMEM((blocks, heads, SPAN), F32),
            pltpu.VMEM((blocks, 8, SPAN), F32),
            pltpu.VMEM((tokens, NSTATE), F32),
            pltpu.VMEM((NSTATE, chans), BF16),
            pltpu.VMEM((1, chans), F32),
            pltpu.VMEM((n_head, chunk, chans), F32),
            pltpu.VMEM((n_head, chunk, chans), F32),
            pltpu.VMEM((2, NSTATE, half), F32),
            pltpu.VMEM((2, 8, half), F32),
            pltpu.VMEM((2, NSTATE + 8, half), F32),
            pltpu.VMEM((NSTATE + 8, half), F32),
            pltpu.VMEM((NSTATE + 8, half), F32),
            pltpu.VMEM((chips, deep + 8, 128), F32),
            pltpu.VMEM((chips, deep + 8, 128), F32),
            pltpu.VMEM((chips, deep, 128), F32),
            pltpu.VMEM((chips, deep, 128), F32),
            pltpu.VMEM((NSTATE, half), F32),
            pltpu.VMEM((NSTATE, half), F32),
            pltpu.VMEM((blocks, 2, NSTATE, half), BF16),
            pltpu.VMEM((chunk, chans), BF16),
            pltpu.VMEM((n_head, PIECES, chunk, width), F32),
            dma((10,)),
            dma((2,)),
            dma((2,)),
            dma((2, chips)),
            dma((2, chips)),
            dma((n_head - 1, PIECES)),
            dma((n_head - 1, PIECES)),
        ]
        return pl.pallas_call(
            functools.partial(kernel, n_ctx, n_head),
            out_shape=jax.ShapeDtypeStruct((chunk, width_out), BF16),
            in_specs=[pl.BlockSpec(memory_space=pl.ANY)] * 10,
            out_specs=pl.BlockSpec(memory_space=pltpu.VMEM),
            scratch_shapes=scratch,
            compiler_params=pltpu.CompilerParams(
                collective_id=0, has_side_effects=True, vmem_limit_bytes=56 * 1024 * 1024
            ),
        )(
            features.reshape(blocks, SPAN, chans),
            gate_values.reshape(blocks, SPAN, chans),
            write_proj.reshape(blocks, SPAN, NSTATE),
            read_proj.reshape(blocks, SPAN, NSTATE),
            step_size,
            log_decay,
            starts.reshape(1, tokens),
            skip_weight.reshape(1, heads),
            norm_gain.reshape(1, chans),
            out_weight,
        )

    placed = (
        P("ctx", "head"),
        P("ctx", "head"),
        P("ctx", "head"),
        P("ctx", "head"),
        P("head", "ctx"),
        P("head", "ctx"),
        P("ctx"),
        P("head"),
        P("head"),
        P("head", None),
    )
    return jax.shard_map(
        body, mesh=mesh, in_specs=placed, out_specs=P(("ctx", "head"), None), check_vma=False
    )
```

```python
import functools

import jax
import jax.numpy as jnp
from jax import lax
from jax.experimental import pallas as pl
from jax.experimental.pallas import tpu as pltpu
from jax.sharding import PartitionSpec as P

MESH = pl.DeviceIdType.MESH
F32 = jnp.float32
BF16 = jnp.bfloat16

HEAD_DIM = 64
NSTATE = 128
SPAN = 256
EPS = 1e-05
MASKED = -1e30
PIECES = 4
EARLY = (4, 4)
FIRST = ("decay", "starts", "step", "write", "feat")


def split3(value):
    high = value.astype(BF16)
    rest = value - high.astype(F32)
    mid = rest.astype(BF16)
    low = (rest - mid.astype(F32)).astype(BF16)
    return high, mid, low


def kernel(
    n_ctx,
    n_head,
    feat_hbm,
    gate_hbm,
    write_hbm,
    read_hbm,
    step_hbm,
    decay_hbm,
    starts_hbm,
    skip_hbm,
    gain_hbm,
    weight_hbm,
    out_ref,
    feat,
    gate,
    write,
    read,
    step,
    decay,
    starts,
    skip,
    gain,
    weight,
    write_t,
    rows_u,
    rows_seg,
    cols,
    expand,
    skip_row,
    ready,
    reach,
    state0,
    keep0,
    total,
    partner_part,
    first_state,
    send1,
    recv1,
    send2,
    recv2,
    send3,
    recv3,
    entry,
    normed,
    ring,
    held,
    in_sem,
    pair_send,
    pair_recv,
    ex_send,
    ex_recv,
    ring_send,
    ring_recv,
):
    ctx = lax.axis_index("ctx")
    z = lax.axis_index("head")
    core = lax.rem(ctx, 2)
    chip = ctx // 2
    chips = n_ctx // 2
    other = ctx + 1 - 2 * core
    heads = step.shape[0]
    blocks, span, chans = feat.shape
    half = chans // 2
    chunk = blocks * span // n_head
    per_block = span // chunk
    width = ring.shape[3]
    target = lax.rem(z + 1 + (n_head - 2) * core, n_head)

    side = 4
    tall = chips // side
    steps = [(i, j) for i in range(tall) for j in range(side) if (i, j) != (0, 0)]
    steps.sort(key=lambda step: -min(step[0], tall - step[0]) - min(step[1], side - step[1]))
    at_x, at_y = chip // side, lax.rem(chip, side)
    peers = [lax.rem(at_x + i, tall) * side + lax.rem(at_y + j, side) for i, j in steps]

    loads = {}
    for index, (name, source, dest) in enumerate(
        [
            ("decay", decay_hbm, decay),
            ("starts", starts_hbm, starts),
            ("step", step_hbm, step),
            ("write", write_hbm, write),
            ("feat", feat_hbm, feat),
            ("read", read_hbm, read),
            ("gate", gate_hbm, gate),
            ("skip", skip_hbm, skip),
            ("gain", gain_hbm, gain),
            ("weight", weight_hbm, weight),
        ]
    ):
        loads[name] = pltpu.make_async_copy(source, dest, in_sem.at[index])
        if name in FIRST:
            loads[name].start()

    barrier = pltpu.get_barrier_semaphore()
    pl.semaphore_signal(barrier, inc=1, device_id={"ctx": other, "head": z}, device_id_type=MESH)
    for offset in (1, n_head - 1):
        pl.semaphore_signal(
            barrier, inc=1, device_id={"ctx": ctx, "head": lax.rem(z + offset, n_head)}, device_id_type=MESH
        )

    for peer in peers:
        pl.semaphore_signal(barrier, inc=1, device_id={"ctx": 2 * peer + core, "head": z}, device_id_type=MESH)

    row_id = lax.broadcasted_iota(jnp.int32, (span, span), 0)
    col_id = lax.broadcasted_iota(jnp.int32, (span, span), 1)
    upto = (row_id <= col_id).astype(F32).astype(BF16)
    head_of = lax.broadcasted_iota(jnp.int32, (heads, chans), 1) // HEAD_DIM
    pick = (head_of == lax.broadcasted_iota(jnp.int32, (heads, chans), 0)).astype(F32)

    def spread(column):
        return jnp.sum(column * pick, axis=0, keepdims=True)

    lane_head = lax.broadcasted_iota(jnp.int32, (1, 256), 1) // HEAD_DIM

    def diagonal(stacked, rows):
        result = stacked[0:rows]
        for i in range(1, 4):
            result = jnp.where(lane_head == i, stacked[i * rows : (i + 1) * rows], result)
        return result

    loads["decay"].wait()
    loads["starts"].wait()
    sums = []
    for k in range(blocks):
        tokens = slice(k * span, (k + 1) * span)
        start_rows = jnp.broadcast_to(starts[:, tokens].astype(F32), (heads, span)).astype(BF16)
        stacked = jnp.concatenate([*split3(decay[:, tokens]), start_rows], axis=0)
        sums.append(jnp.dot(stacked, upto, preferred_element_type=F32))
    loads["step"].wait()
    loads["write"].wait()
    keeps, states, tails, cums, segs = [], [], [], [], []
    for k in range(blocks):
        tokens = slice(k * span, (k + 1) * span)
        cum = sums[k][0:heads] + sums[k][heads : 2 * heads] + sums[k][2 * heads : 3 * heads]
        seg = sums[k][3 * heads : 3 * heads + 1]
        last = cum[:, span - 1 : span]
        seg_last = seg[:, span - 1 : span]
        tails.append(jnp.where(seg == seg_last, jnp.exp(last - cum), 0.0) * step[:, tokens])
        keeps.append(spread(jnp.where(seg_last == 0.0, jnp.exp(last), 0.0)))
        cums.append(cum)
        segs.append(seg)
    loads["feat"].wait()
    for name, load in loads.items():
        if name not in FIRST:
            load.start()
    for k in range(blocks):
        turned = jnp.transpose(write[k].astype(F32))
        write_t[k] = turned.astype(BF16)
        parts = []
        for quad in range(heads // 4):
            lhs = jnp.concatenate(
                [(turned * tails[k][4 * quad + i : 4 * quad + i + 1]).astype(BF16) for i in range(4)], axis=0
            )
            full = jnp.dot(lhs, feat[k, :, 256 * quad : 256 * (quad + 1)], preferred_element_type=F32)
            parts.append(diagonal(full, NSTATE))
        states.append(parts)
    per_half = half // 256
    for h in range(2):
        cut = slice(h * half, (h + 1) * half)
        keep0[h] = jnp.broadcast_to(keeps[0][:, cut], (8, half))
        total[h, NSTATE:] = jnp.broadcast_to((keeps[0] * keeps[1])[:, cut], (8, half))
        for part in range(per_half):
            lanes = slice(256 * part, 256 * (part + 1))
            chans_at = slice(h * half + 256 * part, h * half + 256 * (part + 1))
            first = states[0][h * per_half + part]
            state0[h, :, lanes] = first
            total[h, :NSTATE, lanes] = keeps[1][:, chans_at] * first + states[1][h * per_half + part]

    pl.semaphore_wait(barrier, chips + 2)
    pair1 = pltpu.make_async_remote_copy(
        src_ref=total.at[1 - core],
        dst_ref=partner_part,
        send_sem=pair_send.at[0],
        recv_sem=pair_recv.at[0],
        device_id={"ctx": other, "head": z},
        device_id_type=MESH,
    )
    pair1.start()

    def columns_of_block(k):
        tokens = slice(k * span, (k + 1) * span)
        rows_u[k] = cums[k] - jnp.log(step[:, tokens])
        rows_seg[k] = jnp.broadcast_to(segs[k], (8, span))
        reach_scale = jnp.where(segs[k] == 0.0, jnp.exp(cums[k]), 0.0)
        pieces = [part.astype(F32) for part in split3(reach_scale)]
        seg_rows = jnp.broadcast_to(segs[k], (heads, span))
        pad = jnp.zeros((NSTATE - 5 * heads, span), F32)
        cols[tokens] = jnp.transpose(jnp.concatenate([cums[k], *pieces, seg_rows, pad], axis=0))

    for k in range(blocks):
        columns_of_block(k)
    line = lax.broadcasted_iota(jnp.int32, (NSTATE, chans), 0)
    owner = lax.broadcasted_iota(jnp.int32, (NSTATE, chans), 1) // HEAD_DIM
    inside = (line >= heads) & (line < 4 * heads)
    expand[...] = jnp.where(inside & (lax.rem(line, heads) == owner), 1.0, 0.0).astype(BF16)
    loads["skip"].wait()
    square = jnp.broadcast_to(skip[...], (heads, heads))
    same = lax.broadcasted_iota(jnp.int32, (heads, heads), 0) == lax.broadcasted_iota(jnp.int32, (heads, heads), 1)
    skip_row[...] = spread(jnp.sum(jnp.where(same, square, 0.0), axis=1, keepdims=True))
    ring[0] = jnp.zeros_like(ring[0])

    pair1.wait_recv()
    mine = total[core]
    theirs = partner_part[...]
    leads = core == 0
    s0 = jnp.where(leads, mine[:NSTATE], theirs[:NSTATE])
    s1 = jnp.where(leads, theirs[:NSTATE], mine[:NSTATE])
    m0 = jnp.where(leads, mine[NSTATE:], theirs[NSTATE:])
    m1 = jnp.where(leads, theirs[NSTATE:], mine[NSTATE:])
    first_state[:NSTATE] = s0
    first_state[NSTATE:] = m0
    joined = m1[0:1] * s0 + s1
    joined_mult = m0 * m1
    across = half // 128
    deep = NSTATE // (chips // across)
    for q in range(chips):
        rows = slice(deep * (q // across), deep * (q // across + 1))
        lanes = slice(128 * (q % across), 128 * (q % across + 1))
        send1[q, :deep] = joined[rows, lanes]
        send1[q, deep:] = joined_mult[0:1, lanes]

    for peer in peers:
        pltpu.make_async_remote_copy(
            src_ref=send1.at[peer],
            dst_ref=recv1.at[chip],
            send_sem=ex_send.at[0, peer],
            recv_sem=ex_recv.at[0, chip],
            device_id={"ctx": 2 * peer + core, "head": z},
            device_id_type=MESH,
        ).start()
    recv1[chip] = send1[chip]

    def chunk_of(s):
        return lax.rem(z + (1 - core) * (n_head - 1 - s) + core * (1 + s), n_head)

    loads["read"].wait()
    loads["gate"].wait()
    loads["gain"].wait()

    def prepare(s):
        b = chunk_of(s)
        k = b // per_block
        local = pl.multiple_of(lax.rem(b, per_block) * chunk, chunk)
        at = pl.multiple_of(b * chunk, chunk)
        scores = jnp.dot(read[k, pl.ds(local, chunk), :], write_t[k], preferred_element_type=F32)
        column = cols[pl.ds(at, chunk), :]
        seg_row = rows_seg[k][0:1]
        seg_col = column[:, 4 * heads : 4 * heads + 1]
        later = local + lax.broadcasted_iota(jnp.int32, (chunk, span), 0)
        earlier = lax.broadcasted_iota(jnp.int32, (chunk, span), 1)
        mask = jnp.where((seg_col == seg_row) & (earlier <= later), 0.0, MASKED)
        u = rows_u[k]
        scale = jnp.dot(column.astype(BF16), expand[...], preferred_element_type=F32)
        for quad in range(heads // 4):
            lanes = slice(256 * quad, 256 * (quad + 1))
            stack = []
            for h in range(4 * quad, 4 * quad + 4):
                spread_log = column[:, h : h + 1] - u[h : h + 1] + mask
                stack.append((jnp.exp(spread_log) * scores).astype(BF16))
            full = jnp.dot(jnp.concatenate(stack, axis=0), feat[k, :, lanes], preferred_element_type=F32)
            gates = gate[k, pl.ds(local, chunk), lanes].astype(F32)
            silu = gates * jax.nn.sigmoid(gates)
            direct = skip_row[:, lanes] * feat[k, pl.ds(local, chunk), lanes].astype(F32)
            ready[s, :, lanes] = (diagonal(full, chunk) + direct) * silu
            reach[s, :, lanes] = scale[:, lanes] * silu

    def prepare_loop(low, high):
        def run(s, carry):
            prepare(s)
            return carry

        lax.fori_loop(low, high, run, 0)

    prepare_loop(0, EARLY[0])

    def back(peer):
        return pltpu.make_async_remote_copy(
            src_ref=send2.at[peer],
            dst_ref=recv2.at[chip],
            send_sem=ex_send.at[1, peer],
            recv_sem=ex_recv.at[1, chip],
            device_id={"ctx": 2 * peer + core, "head": z},
            device_id_type=MESH,
        )

    def arrival(round_, peer, dest):
        return pltpu.make_async_remote_copy(
            src_ref=dest.at[peer],
            dst_ref=dest.at[peer],
            send_sem=ex_send.at[round_, peer],
            recv_sem=ex_recv.at[round_, peer],
            device_id={"ctx": 2 * peer + core, "head": z},
            device_id_type=MESH,
        )

    for peer in reversed(peers):
        arrival(0, peer, recv1).wait_recv()
    state = jnp.zeros((deep, 128), F32)
    for p in range(chips):
        send2[p] = state
        state = recv1[p, deep : deep + 1] * state + recv1[p, :deep]
    for peer in peers:
        back(peer).start()
    recv2[chip] = send2[chip]

    prepare_loop(EARLY[0], EARLY[0] + EARLY[1])

    for peer in reversed(peers):
        arrival(1, peer, recv2).wait_recv()
    strips = []
    for down in range(chips // across):
        strips.append(jnp.concatenate([recv2[down * across + right] for right in range(across)], axis=1))
    entry0 = jnp.concatenate(strips, axis=0)
    entry1 = first_state[NSTATE : NSTATE + 1] * entry0 + first_state[:NSTATE]
    send3[...] = jnp.where(leads, entry1, entry0)
    pair2 = pltpu.make_async_remote_copy(
        src_ref=send3,
        dst_ref=recv3,
        send_sem=pair_send.at[1],
        recv_sem=pair_recv.at[1],
        device_id={"ctx": other, "head": z},
        device_id_type=MESH,
    )
    pair2.start()

    def set_entry(h, value):
        entry[0, h] = value.astype(BF16)
        entry[1, h] = (keep0[h][0:1] * value + state0[h]).astype(BF16)

    set_entry(core, jnp.where(leads, entry0, entry1))
    loads["weight"].wait()
    pair2.wait_recv()
    set_entry(1 - core, recv3[...])

    def hop(s, piece):
        return pltpu.make_async_remote_copy(
            src_ref=ring.at[s, piece],
            dst_ref=ring.at[s + 1, piece],
            send_sem=ring_send.at[s, piece],
            recv_sem=ring_recv.at[s, piece],
            device_id={"ctx": ctx, "head": target},
            device_id_type=MESH,
        )

    def normalise(s):
        b = chunk_of(s)
        k = b // per_block
        local = pl.multiple_of(lax.rem(b, per_block) * chunk, chunk)
        reads = read[k, pl.ds(local, chunk), :]
        gated = []
        squares = jnp.zeros((chunk, 1), F32)
        for h in range(2):
            lanes = slice(h * half, (h + 1) * half)
            carried = jnp.dot(reads, entry[k, h], preferred_element_type=F32)
            value = ready[s, :, lanes] + reach[s, :, lanes] * carried
            squares = squares + jnp.sum(value * value, axis=1, keepdims=True)
            gated.append(value)
        scale = lax.rsqrt(squares * (1.0 / chans) + EPS)
        for h in range(2):
            lanes = slice(h * half, (h + 1) * half)
            normed[:, lanes] = (gated[h] * scale * gain[:, lanes]).astype(BF16)

    def product(piece):
        return jnp.dot(normed[...], weight[:, piece * width : (piece + 1) * width], preferred_element_type=F32)

    def ring_step(s, carry):
        normalise(s)
        for piece in range(PIECES):
            own = product(piece)

            @pl.when(s > 0)
            def _():
                hop(s - 1, piece).wait_recv()

            ring[s, piece] = ring[s, piece] + own
            hop(s, piece).start()
        return carry

    last = n_head - 1
    lax.fori_loop(0, last, ring_step, 0)
    normalise(last)
    for piece in range(PIECES):
        held[piece] = product(piece)

    pair1.wait_send()
    pair2.wait_send()
    for peer in peers:
        arrival(0, peer, recv1).wait_send()
        arrival(1, peer, recv2).wait_send()

    def drain(s, carry):
        for piece in range(PIECES):
            hop(s, piece).wait_send()
        return carry

    lax.fori_loop(0, last - 1, drain, 0)
    for piece in range(PIECES):
        hop(last - 1, piece).wait_recv()
        out_ref[:, piece * width : (piece + 1) * width] = (ring[last, piece] + held[piece]).astype(BF16)

    for piece in range(PIECES):
        hop(last - 1, piece).wait_send()


def solution(mesh):
    n_ctx, n_head = mesh.shape["ctx"], mesh.shape["head"]

    def body(features, gate_values, write_proj, read_proj, step_size, log_decay, starts, skip_weight, norm_gain, out_weight):
        tokens, chans = features.shape
        heads = step_size.shape[0]
        blocks = tokens // SPAN
        width_out = out_weight.shape[1]
        chunk = tokens // n_head
        half = chans // 2
        chips = n_ctx // 2
        across = half // 128
        deep = NSTATE // (chips // across)
        width = width_out // PIECES
        dma = pltpu.SemaphoreType.DMA
        scratch = [
            pltpu.VMEM((blocks, SPAN, chans), BF16),
            pltpu.VMEM((blocks, SPAN, chans), BF16),
            pltpu.VMEM((blocks, SPAN, NSTATE), BF16),
            pltpu.VMEM((blocks, SPAN, NSTATE), BF16),
            pltpu.VMEM((heads, tokens), F32),
            pltpu.VMEM((heads, tokens), F32),
            pltpu.VMEM((1, tokens), jnp.int32),
            pltpu.VMEM((1, heads), F32),
            pltpu.VMEM((1, chans), F32),
            pltpu.VMEM((chans, width_out), BF16),
            pltpu.VMEM((blocks, NSTATE, SPAN), BF16),
            pltpu.VMEM((blocks, heads, SPAN), F32),
            pltpu.VMEM((blocks, 8, SPAN), F32),
            pltpu.VMEM((tokens, NSTATE), F32),
            pltpu.VMEM((NSTATE, chans), BF16),
            pltpu.VMEM((1, chans), F32),
            pltpu.VMEM((n_head, chunk, chans), F32),
            pltpu.VMEM((n_head, chunk, chans), F32),
            pltpu.VMEM((2, NSTATE, half), F32),
            pltpu.VMEM((2, 8, half), F32),
            pltpu.VMEM((2, NSTATE + 8, half), F32),
            pltpu.VMEM((NSTATE + 8, half), F32),
            pltpu.VMEM((NSTATE + 8, half), F32),
            pltpu.VMEM((chips, deep + 1, 128), F32),
            pltpu.VMEM((chips, deep + 1, 128), F32),
            pltpu.VMEM((chips, deep, 128), F32),
            pltpu.VMEM((chips, deep, 128), F32),
            pltpu.VMEM((NSTATE, half), F32),
            pltpu.VMEM((NSTATE, half), F32),
            pltpu.VMEM((blocks, 2, NSTATE, half), BF16),
            pltpu.VMEM((chunk, chans), BF16),
            pltpu.VMEM((n_head, PIECES, chunk, width), F32),
            pltpu.VMEM((PIECES, chunk, width), F32),
            dma((10,)),
            dma((2,)),
            dma((2,)),
            dma((2, chips)),
            dma((2, chips)),
            dma((n_head - 1, PIECES)),
            dma((n_head - 1, PIECES)),
        ]
        return pl.pallas_call(
            functools.partial(kernel, n_ctx, n_head),
            out_shape=jax.ShapeDtypeStruct((chunk, width_out), BF16),
            in_specs=[pl.BlockSpec(memory_space=pl.ANY)] * 10,
            out_specs=pl.BlockSpec(memory_space=pltpu.VMEM),
            scratch_shapes=scratch,
            compiler_params=pltpu.CompilerParams(
                collective_id=0, has_side_effects=True, vmem_limit_bytes=56 * 1024 * 1024
            ),
        )(
            features.reshape(blocks, SPAN, chans),
            gate_values.reshape(blocks, SPAN, chans),
            write_proj.reshape(blocks, SPAN, NSTATE),
            read_proj.reshape(blocks, SPAN, NSTATE),
            step_size,
            log_decay,
            starts.reshape(1, tokens),
            skip_weight.reshape(1, heads),
            norm_gain.reshape(1, chans),
            out_weight,
        )

    placed = (
        P("ctx", "head"),
        P("ctx", "head"),
        P("ctx", "head"),
        P("ctx", "head"),
        P("head", "ctx"),
        P("head", "ctx"),
        P("ctx"),
        P("head"),
        P("head"),
        P("head", None),
    )
    return jax.shard_map(
        body, mesh=mesh, in_specs=placed, out_specs=P(("ctx", "head"), None), check_vma=False
    )
```

```python
import functools

import jax
import jax.numpy as jnp
from jax import lax
from jax.experimental import pallas as pl
from jax.experimental.pallas import tpu as pltpu
from jax.sharding import PartitionSpec as P

MESH = pl.DeviceIdType.MESH
F32 = jnp.float32
BF16 = jnp.bfloat16

HEAD_DIM = 64
NSTATE = 128
SPAN = 256
EPS = 1e-05
MASKED = -1e30
PIECES = 4
EARLY = (4, 4)
FIRST = ("decay", "starts", "step", "write", "feat")


def split3(value):
    high = value.astype(BF16)
    rest = value - high.astype(F32)
    mid = rest.astype(BF16)
    low = (rest - mid.astype(F32)).astype(BF16)
    return high, mid, low


def kernel(
    n_ctx,
    n_head,
    feat_hbm,
    gate_hbm,
    write_hbm,
    read_hbm,
    step_hbm,
    decay_hbm,
    starts_hbm,
    skip_hbm,
    gain_hbm,
    weight_hbm,
    out_ref,
    feat,
    gate,
    write,
    read,
    step,
    decay,
    starts,
    skip,
    gain,
    weight,
    write_t,
    rows_u,
    rows_seg,
    cols,
    expand,
    expand_tail,
    skip_row,
    ready,
    reach,
    state0,
    keep0,
    total,
    partner_part,
    first_state,
    send1,
    recv1,
    send2,
    recv2,
    send3,
    recv3,
    entry,
    normed,
    ring,
    held,
    in_sem,
    pair_send,
    pair_recv,
    ex_send,
    ex_recv,
    ring_send,
    ring_recv,
):
    ctx = lax.axis_index("ctx")
    z = lax.axis_index("head")
    core = lax.rem(ctx, 2)
    chip = ctx // 2
    chips = n_ctx // 2
    other = ctx + 1 - 2 * core
    heads = step.shape[0]
    blocks, span, chans = feat.shape
    half = chans // 2
    chunk = blocks * span // n_head
    per_block = span // chunk
    width = ring.shape[3]
    target = lax.rem(z + 1 + (n_head - 2) * core, n_head)

    side = 4
    tall = chips // side
    steps = [(i, j) for i in range(tall) for j in range(side) if (i, j) != (0, 0)]
    steps.sort(key=lambda step: -min(step[0], tall - step[0]) - min(step[1], side - step[1]))
    at_x, at_y = chip // side, lax.rem(chip, side)
    peers = [lax.rem(at_x + i, tall) * side + lax.rem(at_y + j, side) for i, j in steps]

    loads = {}
    for index, (name, source, dest) in enumerate(
        [
            ("decay", decay_hbm, decay),
            ("starts", starts_hbm, starts),
            ("step", step_hbm, step),
            ("write", write_hbm, write),
            ("feat", feat_hbm, feat),
            ("read", read_hbm, read),
            ("gate", gate_hbm, gate),
            ("skip", skip_hbm, skip),
            ("gain", gain_hbm, gain),
            ("weight", weight_hbm, weight),
        ]
    ):
        loads[name] = pltpu.make_async_copy(source, dest, in_sem.at[index])
        if name in FIRST:
            loads[name].start()

    barrier = pltpu.get_barrier_semaphore()
    pl.semaphore_signal(barrier, inc=1, device_id={"ctx": other, "head": z}, device_id_type=MESH)
    for offset in (1, n_head - 1):
        pl.semaphore_signal(
            barrier, inc=1, device_id={"ctx": ctx, "head": lax.rem(z + offset, n_head)}, device_id_type=MESH
        )

    for peer in peers:
        pl.semaphore_signal(barrier, inc=1, device_id={"ctx": 2 * peer + core, "head": z}, device_id_type=MESH)

    row_id = lax.broadcasted_iota(jnp.int32, (span, span), 0)
    col_id = lax.broadcasted_iota(jnp.int32, (span, span), 1)
    upto = (row_id <= col_id).astype(F32).astype(BF16)
    head_of = lax.broadcasted_iota(jnp.int32, (heads, chans), 1) // HEAD_DIM
    pick = (head_of == lax.broadcasted_iota(jnp.int32, (heads, chans), 0)).astype(F32)

    def spread(column):
        return jnp.sum(column * pick, axis=0, keepdims=True)

    lane_head = lax.broadcasted_iota(jnp.int32, (1, 256), 1) // HEAD_DIM

    def diagonal(stacked, rows):
        result = stacked[0:rows]
        for i in range(1, 4):
            result = jnp.where(lane_head == i, stacked[i * rows : (i + 1) * rows], result)
        return result

    line = lax.broadcasted_iota(jnp.int32, (NSTATE, chans), 0)
    owner = lax.broadcasted_iota(jnp.int32, (NSTATE, chans), 1) // HEAD_DIM
    own_line = lax.rem(line, heads) == owner
    expand_tail[...] = jnp.where(own_line & (line >= 5 * heads), 1.0, 0.0).astype(BF16)

    loads["decay"].wait()
    loads["starts"].wait()
    sums = []
    for k in range(blocks):
        tokens = slice(k * span, (k + 1) * span)
        start_rows = jnp.broadcast_to(starts[:, tokens].astype(F32), (heads, span)).astype(BF16)
        stacked = jnp.concatenate([*split3(decay[:, tokens]), start_rows], axis=0)
        sums.append(jnp.dot(stacked, upto, preferred_element_type=F32))
    loads["step"].wait()
    loads["write"].wait()
    keeps, states, cums, segs = [], [], [], []
    for k in range(blocks):
        tokens = slice(k * span, (k + 1) * span)
        cum = sums[k][0:heads] + sums[k][heads : 2 * heads] + sums[k][2 * heads : 3 * heads]
        seg = sums[k][3 * heads : 3 * heads + 1]
        last = cum[:, span - 1 : span]
        seg_last = seg[:, span - 1 : span]
        tail = jnp.where(seg == seg_last, jnp.exp(last - cum), 0.0) * step[:, tokens]
        reach_scale = jnp.where(seg == 0.0, jnp.exp(cum), 0.0)
        reach_parts = [part.astype(F32) for part in split3(reach_scale)]
        tail_parts = [part.astype(F32) for part in split3(tail)]
        seg_rows = jnp.broadcast_to(seg, (heads, span))
        cols[tokens] = jnp.transpose(jnp.concatenate([cum, *reach_parts, seg_rows, *tail_parts], axis=0))
        keeps.append(spread(jnp.where(seg_last == 0.0, jnp.exp(last), 0.0)))
        cums.append(cum)
        segs.append(seg)
    loads["feat"].wait()
    for name, load in loads.items():
        if name not in FIRST:
            load.start()
    for k in range(blocks):
        write_t[k] = jnp.transpose(write[k].astype(F32)).astype(BF16)
        column = cols[k * span : (k + 1) * span].astype(BF16)
        parts = []
        for quad in range(heads // 4):
            lanes = slice(256 * quad, 256 * (quad + 1))
            tail = jnp.dot(column, expand_tail[:, lanes], preferred_element_type=F32)
            scaled = (tail * feat[k, :, lanes].astype(F32)).astype(BF16)
            parts.append(jnp.dot(write_t[k], scaled, preferred_element_type=F32))
        states.append(parts)
    per_half = half // 256
    for h in range(2):
        cut = slice(h * half, (h + 1) * half)
        keep0[h] = jnp.broadcast_to(keeps[0][:, cut], (8, half))
        total[h, NSTATE:] = jnp.broadcast_to((keeps[0] * keeps[1])[:, cut], (8, half))
        for part in range(per_half):
            lanes = slice(256 * part, 256 * (part + 1))
            chans_at = slice(h * half + 256 * part, h * half + 256 * (part + 1))
            first = states[0][h * per_half + part]
            state0[h, :, lanes] = first
            total[h, :NSTATE, lanes] = keeps[1][:, chans_at] * first + states[1][h * per_half + part]

    pl.semaphore_wait(barrier, chips + 2)
    pair1 = pltpu.make_async_remote_copy(
        src_ref=total.at[1 - core],
        dst_ref=partner_part,
        send_sem=pair_send.at[0],
        recv_sem=pair_recv.at[0],
        device_id={"ctx": other, "head": z},
        device_id_type=MESH,
    )
    pair1.start()

    pair1.wait_recv()
    mine = total[core]
    theirs = partner_part[...]
    leads = core == 0
    s0 = jnp.where(leads, mine[:NSTATE], theirs[:NSTATE])
    s1 = jnp.where(leads, theirs[:NSTATE], mine[:NSTATE])
    m0 = jnp.where(leads, mine[NSTATE:], theirs[NSTATE:])
    m1 = jnp.where(leads, theirs[NSTATE:], mine[NSTATE:])
    first_state[:NSTATE] = s0
    first_state[NSTATE:] = m0
    joined = m1[0:1] * s0 + s1
    joined_mult = m0 * m1
    across = half // 128
    deep = NSTATE // (chips // across)
    for q in range(chips):
        rows = slice(deep * (q // across), deep * (q // across + 1))
        lanes = slice(128 * (q % across), 128 * (q % across + 1))
        send1[q, :deep] = joined[rows, lanes]
        send1[q, deep:] = joined_mult[0:1, lanes]

    for peer in peers:
        pltpu.make_async_remote_copy(
            src_ref=send1.at[peer],
            dst_ref=recv1.at[chip],
            send_sem=ex_send.at[0, peer],
            recv_sem=ex_recv.at[0, chip],
            device_id={"ctx": 2 * peer + core, "head": z},
            device_id_type=MESH,
        ).start()
    recv1[chip] = send1[chip]

    def rows_of_block(k):
        tokens = slice(k * span, (k + 1) * span)
        rows_u[k] = cums[k] - jnp.log(step[:, tokens])
        rows_seg[k] = jnp.broadcast_to(segs[k], (8, span))

    for k in range(blocks):
        rows_of_block(k)
    loads["skip"].wait()
    square = jnp.broadcast_to(skip[...], (heads, heads))
    same = lax.broadcasted_iota(jnp.int32, (heads, heads), 0) == lax.broadcasted_iota(jnp.int32, (heads, heads), 1)
    skip_row[...] = spread(jnp.sum(jnp.where(same, square, 0.0), axis=1, keepdims=True))
    expand[...] = jnp.where(own_line & (line >= heads) & (line < 4 * heads), 1.0, 0.0).astype(BF16)
    ring[0] = jnp.zeros_like(ring[0])


    def chunk_of(s):
        return lax.rem(z + (1 - core) * (n_head - 1 - s) + core * (1 + s), n_head)

    loads["read"].wait()
    loads["gate"].wait()
    loads["gain"].wait()

    def prepare(s):
        b = chunk_of(s)
        k = b // per_block
        local = pl.multiple_of(lax.rem(b, per_block) * chunk, chunk)
        at = pl.multiple_of(b * chunk, chunk)
        scores = jnp.dot(read[k, pl.ds(local, chunk), :], write_t[k], preferred_element_type=F32)
        column = cols[pl.ds(at, chunk), :]
        seg_row = rows_seg[k][0:1]
        seg_col = column[:, 4 * heads : 4 * heads + 1]
        later = local + lax.broadcasted_iota(jnp.int32, (chunk, span), 0)
        earlier = lax.broadcasted_iota(jnp.int32, (chunk, span), 1)
        mask = jnp.where((seg_col == seg_row) & (earlier <= later), 0.0, MASKED)
        u = rows_u[k]
        scale = jnp.dot(column.astype(BF16), expand[...], preferred_element_type=F32)
        for quad in range(heads // 4):
            lanes = slice(256 * quad, 256 * (quad + 1))
            stack = []
            for h in range(4 * quad, 4 * quad + 4):
                spread_log = column[:, h : h + 1] - u[h : h + 1] + mask
                stack.append((jnp.exp(spread_log) * scores).astype(BF16))
            full = jnp.dot(jnp.concatenate(stack, axis=0), feat[k, :, lanes], preferred_element_type=F32)
            gates = gate[k, pl.ds(local, chunk), lanes].astype(F32)
            silu = gates * jax.nn.sigmoid(gates)
            direct = skip_row[:, lanes] * feat[k, pl.ds(local, chunk), lanes].astype(F32)
            ready[s, :, lanes] = (diagonal(full, chunk) + direct) * silu
            reach[s, :, lanes] = scale[:, lanes] * silu

    def prepare_loop(low, high):
        def run(s, carry):
            prepare(s)
            return carry

        lax.fori_loop(low, high, run, 0)

    prepare_loop(0, EARLY[0])

    def back(peer):
        return pltpu.make_async_remote_copy(
            src_ref=send2.at[peer],
            dst_ref=recv2.at[chip],
            send_sem=ex_send.at[1, peer],
            recv_sem=ex_recv.at[1, chip],
            device_id={"ctx": 2 * peer + core, "head": z},
            device_id_type=MESH,
        )

    def arrival(round_, peer, dest):
        return pltpu.make_async_remote_copy(
            src_ref=dest.at[peer],
            dst_ref=dest.at[peer],
            send_sem=ex_send.at[round_, peer],
            recv_sem=ex_recv.at[round_, peer],
            device_id={"ctx": 2 * peer + core, "head": z},
            device_id_type=MESH,
        )

    for peer in reversed(peers):
        arrival(0, peer, recv1).wait_recv()
    state = jnp.zeros((deep, 128), F32)
    for p in range(chips):
        send2[p] = state
        state = recv1[p, deep : deep + 1] * state + recv1[p, :deep]
    for peer in peers:
        back(peer).start()
    recv2[chip] = send2[chip]

    prepare_loop(EARLY[0], EARLY[0] + EARLY[1])

    for peer in reversed(peers):
        arrival(1, peer, recv2).wait_recv()
    strips = []
    for down in range(chips // across):
        strips.append(jnp.concatenate([recv2[down * across + right] for right in range(across)], axis=1))
    entry0 = jnp.concatenate(strips, axis=0)
    entry1 = first_state[NSTATE : NSTATE + 1] * entry0 + first_state[:NSTATE]
    send3[...] = jnp.where(leads, entry1, entry0)
    pair2 = pltpu.make_async_remote_copy(
        src_ref=send3,
        dst_ref=recv3,
        send_sem=pair_send.at[1],
        recv_sem=pair_recv.at[1],
        device_id={"ctx": other, "head": z},
        device_id_type=MESH,
    )
    pair2.start()

    def set_entry(h, value):
        entry[0, h] = value.astype(BF16)
        entry[1, h] = (keep0[h][0:1] * value + state0[h]).astype(BF16)

    set_entry(core, jnp.where(leads, entry0, entry1))
    loads["weight"].wait()
    pair2.wait_recv()
    set_entry(1 - core, recv3[...])

    def hop(s, piece):
        return pltpu.make_async_remote_copy(
            src_ref=ring.at[s, piece],
            dst_ref=ring.at[s + 1, piece],
            send_sem=ring_send.at[s, piece],
            recv_sem=ring_recv.at[s, piece],
            device_id={"ctx": ctx, "head": target},
            device_id_type=MESH,
        )

    def normalise(s):
        b = chunk_of(s)
        k = b // per_block
        local = pl.multiple_of(lax.rem(b, per_block) * chunk, chunk)
        reads = read[k, pl.ds(local, chunk), :]
        gated = []
        squares = jnp.zeros((chunk, 1), F32)
        for h in range(2):
            lanes = slice(h * half, (h + 1) * half)
            carried = jnp.dot(reads, entry[k, h], preferred_element_type=F32)
            value = ready[s, :, lanes] + reach[s, :, lanes] * carried
            squares = squares + jnp.sum(value * value, axis=1, keepdims=True)
            gated.append(value)
        scale = lax.rsqrt(squares * (1.0 / chans) + EPS)
        for h in range(2):
            lanes = slice(h * half, (h + 1) * half)
            normed[:, lanes] = (gated[h] * scale * gain[:, lanes]).astype(BF16)

    def product(piece):
        return jnp.dot(normed[...], weight[:, piece * width : (piece + 1) * width], preferred_element_type=F32)

    def ring_step(s, carry):
        normalise(s)
        for piece in range(PIECES):
            own = product(piece)

            @pl.when(s > 0)
            def _():
                hop(s - 1, piece).wait_recv()

            ring[s, piece] = ring[s, piece] + own
            hop(s, piece).start()
        return carry

    last = n_head - 1
    lax.fori_loop(0, last, ring_step, 0)
    normalise(last)
    for piece in range(PIECES):
        held[piece] = product(piece)

    pair1.wait_send()
    pair2.wait_send()
    for peer in peers:
        arrival(0, peer, recv1).wait_send()
        arrival(1, peer, recv2).wait_send()

    def drain(s, carry):
        for piece in range(PIECES):
            hop(s, piece).wait_send()
        return carry

    lax.fori_loop(0, last - 1, drain, 0)
    for piece in range(PIECES):
        hop(last - 1, piece).wait_recv()
        out_ref[:, piece * width : (piece + 1) * width] = (ring[last, piece] + held[piece]).astype(BF16)

    for piece in range(PIECES):
        hop(last - 1, piece).wait_send()


def solution(mesh):
    n_ctx, n_head = mesh.shape["ctx"], mesh.shape["head"]

    def body(features, gate_values, write_proj, read_proj, step_size, log_decay, starts, skip_weight, norm_gain, out_weight):
        tokens, chans = features.shape
        heads = step_size.shape[0]
        blocks = tokens // SPAN
        width_out = out_weight.shape[1]
        chunk = tokens // n_head
        half = chans // 2
        chips = n_ctx // 2
        across = half // 128
        deep = NSTATE // (chips // across)
        width = width_out // PIECES
        dma = pltpu.SemaphoreType.DMA
        scratch = [
            pltpu.VMEM((blocks, SPAN, chans), BF16),
            pltpu.VMEM((blocks, SPAN, chans), BF16),
            pltpu.VMEM((blocks, SPAN, NSTATE), BF16),
            pltpu.VMEM((blocks, SPAN, NSTATE), BF16),
            pltpu.VMEM((heads, tokens), F32),
            pltpu.VMEM((heads, tokens), F32),
            pltpu.VMEM((1, tokens), jnp.int32),
            pltpu.VMEM((1, heads), F32),
            pltpu.VMEM((1, chans), F32),
            pltpu.VMEM((chans, width_out), BF16),
            pltpu.VMEM((blocks, NSTATE, SPAN), BF16),
            pltpu.VMEM((blocks, heads, SPAN), F32),
            pltpu.VMEM((blocks, 8, SPAN), F32),
            pltpu.VMEM((tokens, NSTATE), F32),
            pltpu.VMEM((NSTATE, chans), BF16),
            pltpu.VMEM((NSTATE, chans), BF16),
            pltpu.VMEM((1, chans), F32),
            pltpu.VMEM((n_head, chunk, chans), F32),
            pltpu.VMEM((n_head, chunk, chans), F32),
            pltpu.VMEM((2, NSTATE, half), F32),
            pltpu.VMEM((2, 8, half), F32),
            pltpu.VMEM((2, NSTATE + 8, half), F32),
            pltpu.VMEM((NSTATE + 8, half), F32),
            pltpu.VMEM((NSTATE + 8, half), F32),
            pltpu.VMEM((chips, deep + 1, 128), F32),
            pltpu.VMEM((chips, deep + 1, 128), F32),
            pltpu.VMEM((chips, deep, 128), F32),
            pltpu.VMEM((chips, deep, 128), F32),
            pltpu.VMEM((NSTATE, half), F32),
            pltpu.VMEM((NSTATE, half), F32),
            pltpu.VMEM((blocks, 2, NSTATE, half), BF16),
            pltpu.VMEM((chunk, chans), BF16),
            pltpu.VMEM((n_head, PIECES, chunk, width), F32),
            pltpu.VMEM((PIECES, chunk, width), F32),
            dma((10,)),
            dma((2,)),
            dma((2,)),
            dma((2, chips)),
            dma((2, chips)),
            dma((n_head - 1, PIECES)),
            dma((n_head - 1, PIECES)),
        ]
        return pl.pallas_call(
            functools.partial(kernel, n_ctx, n_head),
            out_shape=jax.ShapeDtypeStruct((chunk, width_out), BF16),
            in_specs=[pl.BlockSpec(memory_space=pltpu.HBM)] * 10,
            out_specs=pl.BlockSpec(memory_space=pltpu.VMEM),
            scratch_shapes=scratch,
            compiler_params=pltpu.CompilerParams(
                collective_id=0, has_side_effects=True, vmem_limit_bytes=48 * 1024 * 1024
            ),
        )(
            *(
                pltpu.with_memory_space_constraint(value, pltpu.HBM)
                for value in (
                    features.reshape(blocks, SPAN, chans),
                    gate_values.reshape(blocks, SPAN, chans),
                    write_proj.reshape(blocks, SPAN, NSTATE),
                    read_proj.reshape(blocks, SPAN, NSTATE),
                    step_size,
                    log_decay,
                    starts.reshape(1, tokens),
                    skip_weight.reshape(1, heads),
                    norm_gain.reshape(1, chans),
                    out_weight,
                )
            )
        )

    placed = (
        P("ctx", "head"),
        P("ctx", "head"),
        P("ctx", "head"),
        P("ctx", "head"),
        P("head", "ctx"),
        P("head", "ctx"),
        P("ctx"),
        P("head"),
        P("head"),
        P("head", None),
    )
    return jax.shard_map(
        body, mesh=mesh, in_specs=placed, out_specs=P(("ctx", "head"), None), check_vma=False
    )
```

```python
import functools

import jax
import jax.numpy as jnp
from jax import lax
from jax.experimental import pallas as pl
from jax.experimental.pallas import tpu as pltpu
from jax.sharding import PartitionSpec as P

MESH = pl.DeviceIdType.MESH
F32 = jnp.float32
BF16 = jnp.bfloat16

HEAD_DIM = 64
NSTATE = 128
SPAN = 256
EPS = 1e-05
MASKED = -1e30
PIECES = 4
EARLY = (4, 4)
FIRST = ("decay", "starts", "step", "write", "feat")


def split3(value):
    high = value.astype(BF16)
    rest = value - high.astype(F32)
    mid = rest.astype(BF16)
    low = (rest - mid.astype(F32)).astype(BF16)
    return high, mid, low


def kernel(
    n_ctx,
    n_head,
    feat_hbm,
    gate_hbm,
    write_hbm,
    read_hbm,
    step_hbm,
    decay_hbm,
    starts_hbm,
    skip_hbm,
    gain_hbm,
    weight_hbm,
    out_ref,
    feat,
    gate,
    write,
    read,
    step,
    decay,
    starts,
    skip,
    gain,
    weight,
    write_t,
    rows_u,
    rows_seg,
    cols,
    expand,
    skip_row,
    ready,
    reach,
    state0,
    keep0,
    total,
    partner_part,
    first_state,
    send1,
    recv1,
    send2,
    recv2,
    send3,
    recv3,
    entry,
    normed,
    ring,
    held,
    in_sem,
    pair_send,
    pair_recv,
    ex_send,
    ex_recv,
    ring_send,
    ring_recv,
):
    ctx = lax.axis_index("ctx")
    z = lax.axis_index("head")
    core = lax.rem(ctx, 2)
    chip = ctx // 2
    chips = n_ctx // 2
    other = ctx + 1 - 2 * core
    heads = step.shape[0]
    blocks, span, chans = feat.shape
    half = chans // 2
    chunk = blocks * span // n_head
    per_block = span // chunk
    width = ring.shape[3]
    target = lax.rem(z + 1 + (n_head - 2) * core, n_head)

    side = 4
    tall = chips // side
    steps = [(i, j) for i in range(tall) for j in range(side) if (i, j) != (0, 0)]
    steps.sort(key=lambda step: -min(step[0], tall - step[0]) - min(step[1], side - step[1]))
    at_x, at_y = chip // side, lax.rem(chip, side)
    peers = [lax.rem(at_x + i, tall) * side + lax.rem(at_y + j, side) for i, j in steps]

    loads = {}
    for index, (name, source, dest) in enumerate(
        [
            ("decay", decay_hbm, decay),
            ("starts", starts_hbm, starts),
            ("step", step_hbm, step),
            ("write", write_hbm, write),
            ("feat", feat_hbm, feat),
            ("read", read_hbm, read),
            ("gate", gate_hbm, gate),
            ("skip", skip_hbm, skip),
            ("gain", gain_hbm, gain),
            ("weight", weight_hbm, weight),
        ]
    ):
        loads[name] = pltpu.make_async_copy(source, dest, in_sem.at[index])
        if name in FIRST:
            loads[name].start()

    barrier = pltpu.get_barrier_semaphore()
    pl.semaphore_signal(barrier, inc=1, device_id={"ctx": other, "head": z}, device_id_type=MESH)
    for offset in (1, n_head - 1):
        pl.semaphore_signal(
            barrier, inc=1, device_id={"ctx": ctx, "head": lax.rem(z + offset, n_head)}, device_id_type=MESH
        )

    for peer in peers:
        pl.semaphore_signal(barrier, inc=1, device_id={"ctx": 2 * peer + core, "head": z}, device_id_type=MESH)

    row_id = lax.broadcasted_iota(jnp.int32, (span, span), 0)
    col_id = lax.broadcasted_iota(jnp.int32, (span, span), 1)
    upto = (row_id <= col_id).astype(F32).astype(BF16)
    head_of = lax.broadcasted_iota(jnp.int32, (heads, chans), 1) // HEAD_DIM
    pick = (head_of == lax.broadcasted_iota(jnp.int32, (heads, chans), 0)).astype(F32)

    def spread(column):
        return jnp.sum(column * pick, axis=0, keepdims=True)

    lane_head = lax.broadcasted_iota(jnp.int32, (1, 256), 1) // HEAD_DIM

    def diagonal(stacked, rows):
        result = stacked[0:rows]
        for i in range(1, 4):
            result = jnp.where(lane_head == i, stacked[i * rows : (i + 1) * rows], result)
        return result

    loads["decay"].wait()
    loads["starts"].wait()
    sums = []
    for k in range(blocks):
        tokens = slice(k * span, (k + 1) * span)
        start_rows = jnp.broadcast_to(starts[:, tokens].astype(F32), (heads, span)).astype(BF16)
        stacked = jnp.concatenate([*split3(decay[:, tokens]), start_rows], axis=0)
        sums.append(jnp.dot(stacked, upto, preferred_element_type=F32))
    loads["step"].wait()
    loads["write"].wait()
    keeps, states, tails, cums, segs = [], [], [], [], []
    for k in range(blocks):
        tokens = slice(k * span, (k + 1) * span)
        cum = sums[k][0:heads] + sums[k][heads : 2 * heads] + sums[k][2 * heads : 3 * heads]
        seg = sums[k][3 * heads : 3 * heads + 1]
        last = cum[:, span - 1 : span]
        seg_last = seg[:, span - 1 : span]
        tails.append(jnp.where(seg == seg_last, jnp.exp(last - cum), 0.0) * step[:, tokens])
        keeps.append(spread(jnp.where(seg_last == 0.0, jnp.exp(last), 0.0)))
        cums.append(cum)
        segs.append(seg)
    loads["feat"].wait()
    for name, load in loads.items():
        if name not in FIRST:
            load.start()
    for k in range(blocks):
        turned = jnp.transpose(write[k].astype(F32))
        write_t[k] = turned.astype(BF16)
        parts = []
        for quad in range(heads // 4):
            lhs = jnp.concatenate(
                [(turned * tails[k][4 * quad + i : 4 * quad + i + 1]).astype(BF16) for i in range(4)], axis=0
            )
            full = jnp.dot(lhs, feat[k, :, 256 * quad : 256 * (quad + 1)], preferred_element_type=F32)
            parts.append(diagonal(full, NSTATE))
        states.append(parts)
    per_half = half // 256
    for h in range(2):
        cut = slice(h * half, (h + 1) * half)
        keep0[h] = jnp.broadcast_to(keeps[0][:, cut], (8, half))
        total[h, NSTATE:] = jnp.broadcast_to((keeps[0] * keeps[1])[:, cut], (8, half))
        for part in range(per_half):
            lanes = slice(256 * part, 256 * (part + 1))
            chans_at = slice(h * half + 256 * part, h * half + 256 * (part + 1))
            first = states[0][h * per_half + part]
            state0[h, :, lanes] = first
            total[h, :NSTATE, lanes] = keeps[1][:, chans_at] * first + states[1][h * per_half + part]

    pl.semaphore_wait(barrier, chips + 2)
    pair1 = pltpu.make_async_remote_copy(
        src_ref=total.at[1 - core],
        dst_ref=partner_part,
        send_sem=pair_send.at[0],
        recv_sem=pair_recv.at[0],
        device_id={"ctx": other, "head": z},
        device_id_type=MESH,
    )
    pair1.start()

    pair1.wait_recv()
    mine = total[core]
    theirs = partner_part[...]
    leads = core == 0
    s0 = jnp.where(leads, mine[:NSTATE], theirs[:NSTATE])
    s1 = jnp.where(leads, theirs[:NSTATE], mine[:NSTATE])
    m0 = jnp.where(leads, mine[NSTATE:], theirs[NSTATE:])
    m1 = jnp.where(leads, theirs[NSTATE:], mine[NSTATE:])
    first_state[:NSTATE] = s0
    first_state[NSTATE:] = m0
    joined = m1[0:1] * s0 + s1
    joined_mult = m0 * m1
    across = half // 128
    deep = NSTATE // (chips // across)
    for q in range(chips):
        rows = slice(deep * (q // across), deep * (q // across + 1))
        lanes = slice(128 * (q % across), 128 * (q % across + 1))
        send1[q, :deep] = joined[rows, lanes]
        send1[q, deep:] = joined_mult[0:1, lanes]

    for peer in peers:
        pltpu.make_async_remote_copy(
            src_ref=send1.at[peer],
            dst_ref=recv1.at[chip],
            send_sem=ex_send.at[0, peer],
            recv_sem=ex_recv.at[0, chip],
            device_id={"ctx": 2 * peer + core, "head": z},
            device_id_type=MESH,
        ).start()
    recv1[chip] = send1[chip]

    def columns_of_block(k):
        tokens = slice(k * span, (k + 1) * span)
        rows_u[k] = cums[k] - jnp.log(step[:, tokens])
        rows_seg[k] = jnp.broadcast_to(segs[k], (8, span))
        reach_scale = jnp.where(segs[k] == 0.0, jnp.exp(cums[k]), 0.0)
        pieces = [part.astype(F32) for part in split3(reach_scale)]
        seg_rows = jnp.broadcast_to(segs[k], (heads, span))
        pad = jnp.zeros((NSTATE - 5 * heads, span), F32)
        cols[tokens] = jnp.transpose(jnp.concatenate([cums[k], *pieces, seg_rows, pad], axis=0))

    for k in range(blocks):
        columns_of_block(k)
    line = lax.broadcasted_iota(jnp.int32, (NSTATE, chans), 0)
    owner = lax.broadcasted_iota(jnp.int32, (NSTATE, chans), 1) // HEAD_DIM
    inside = (line >= heads) & (line < 4 * heads)
    expand[...] = jnp.where(inside & (lax.rem(line, heads) == owner), 1.0, 0.0).astype(BF16)
    loads["skip"].wait()
    square = jnp.broadcast_to(skip[...], (heads, heads))
    same = lax.broadcasted_iota(jnp.int32, (heads, heads), 0) == lax.broadcasted_iota(jnp.int32, (heads, heads), 1)
    skip_row[...] = spread(jnp.sum(jnp.where(same, square, 0.0), axis=1, keepdims=True))
    ring[0] = jnp.zeros_like(ring[0])


    def chunk_of(s):
        return lax.rem(z + (1 - core) * (n_head - 1 - s) + core * (1 + s), n_head)

    loads["read"].wait()
    loads["gate"].wait()
    loads["gain"].wait()

    def prepare(s):
        b = chunk_of(s)
        k = b // per_block
        local = pl.multiple_of(lax.rem(b, per_block) * chunk, chunk)
        at = pl.multiple_of(b * chunk, chunk)
        scores = jnp.dot(read[k, pl.ds(local, chunk), :], write_t[k], preferred_element_type=F32)
        column = cols[pl.ds(at, chunk), :]
        seg_row = rows_seg[k][0:1]
        seg_col = column[:, 4 * heads : 4 * heads + 1]
        later = local + lax.broadcasted_iota(jnp.int32, (chunk, span), 0)
        earlier = lax.broadcasted_iota(jnp.int32, (chunk, span), 1)
        mask = jnp.where((seg_col == seg_row) & (earlier <= later), 0.0, MASKED)
        u = rows_u[k]
        scale = jnp.dot(column.astype(BF16), expand[...], preferred_element_type=F32)
        for quad in range(heads // 4):
            lanes = slice(256 * quad, 256 * (quad + 1))
            stack = []
            for h in range(4 * quad, 4 * quad + 4):
                spread_log = column[:, h : h + 1] - u[h : h + 1] + mask
                stack.append((jnp.exp(spread_log) * scores).astype(BF16))
            full = jnp.dot(jnp.concatenate(stack, axis=0), feat[k, :, lanes], preferred_element_type=F32)
            gates = gate[k, pl.ds(local, chunk), lanes].astype(F32)
            silu = gates * jax.nn.sigmoid(gates)
            direct = skip_row[:, lanes] * feat[k, pl.ds(local, chunk), lanes].astype(F32)
            ready[s, :, lanes] = (diagonal(full, chunk) + direct) * silu
            reach[s, :, lanes] = scale[:, lanes] * silu

    def prepare_loop(low, high):
        def run(s, carry):
            prepare(s)
            return carry

        lax.fori_loop(low, high, run, 0)

    prepare_loop(0, EARLY[0])

    def back(peer):
        return pltpu.make_async_remote_copy(
            src_ref=send2.at[peer],
            dst_ref=recv2.at[chip],
            send_sem=ex_send.at[1, peer],
            recv_sem=ex_recv.at[1, chip],
            device_id={"ctx": 2 * peer + core, "head": z},
            device_id_type=MESH,
        )

    def arrival(round_, peer, dest):
        return pltpu.make_async_remote_copy(
            src_ref=dest.at[peer],
            dst_ref=dest.at[peer],
            send_sem=ex_send.at[round_, peer],
            recv_sem=ex_recv.at[round_, peer],
            device_id={"ctx": 2 * peer + core, "head": z},
            device_id_type=MESH,
        )

    for peer in reversed(peers):
        arrival(0, peer, recv1).wait_recv()
    state = jnp.zeros((deep, 128), F32)
    for p in range(chips):
        send2[p] = state
        state = recv1[p, deep : deep + 1] * state + recv1[p, :deep]
    for peer in peers:
        back(peer).start()
    recv2[chip] = send2[chip]

    prepare_loop(EARLY[0], EARLY[0] + EARLY[1])

    for peer in reversed(peers):
        arrival(1, peer, recv2).wait_recv()
    strips = []
    for down in range(chips // across):
        strips.append(jnp.concatenate([recv2[down * across + right] for right in range(across)], axis=1))
    entry0 = jnp.concatenate(strips, axis=0)
    entry1 = first_state[NSTATE : NSTATE + 1] * entry0 + first_state[:NSTATE]
    send3[...] = jnp.where(leads, entry1, entry0)
    pair2 = pltpu.make_async_remote_copy(
        src_ref=send3,
        dst_ref=recv3,
        send_sem=pair_send.at[1],
        recv_sem=pair_recv.at[1],
        device_id={"ctx": other, "head": z},
        device_id_type=MESH,
    )
    pair2.start()

    def set_entry(h, value):
        entry[0, h] = value.astype(BF16)
        entry[1, h] = (keep0[h][0:1] * value + state0[h]).astype(BF16)

    set_entry(core, jnp.where(leads, entry0, entry1))
    loads["weight"].wait()
    pair2.wait_recv()
    set_entry(1 - core, recv3[...])

    def hop(s, piece):
        return pltpu.make_async_remote_copy(
            src_ref=ring.at[s, piece],
            dst_ref=ring.at[s + 1, piece],
            send_sem=ring_send.at[s, piece],
            recv_sem=ring_recv.at[s, piece],
            device_id={"ctx": ctx, "head": target},
            device_id_type=MESH,
        )

    def normalise(s):
        b = chunk_of(s)
        k = b // per_block
        local = pl.multiple_of(lax.rem(b, per_block) * chunk, chunk)
        reads = read[k, pl.ds(local, chunk), :]
        gated = []
        squares = jnp.zeros((chunk, 1), F32)
        for h in range(2):
            lanes = slice(h * half, (h + 1) * half)
            carried = jnp.dot(reads, entry[k, h], preferred_element_type=F32)
            value = ready[s, :, lanes] + reach[s, :, lanes] * carried
            squares = squares + jnp.sum(value * value, axis=1, keepdims=True)
            gated.append(value)
        scale = lax.rsqrt(squares * (1.0 / chans) + EPS)
        for h in range(2):
            lanes = slice(h * half, (h + 1) * half)
            normed[:, lanes] = (gated[h] * scale * gain[:, lanes]).astype(BF16)

    def product(piece):
        return jnp.dot(normed[...], weight[:, piece * width : (piece + 1) * width], preferred_element_type=F32)

    def ring_step(s, carry):
        normalise(s)
        for piece in range(PIECES):
            own = product(piece)

            @pl.when(s > 0)
            def _():
                hop(s - 1, piece).wait_recv()

            ring[s, piece] = ring[s, piece] + own
            hop(s, piece).start()
        return carry

    last = n_head - 1
    lax.fori_loop(0, last, ring_step, 0)
    normalise(last)
    for piece in range(PIECES):
        held[piece] = product(piece)

    pair1.wait_send()
    pair2.wait_send()
    for peer in peers:
        arrival(0, peer, recv1).wait_send()
        arrival(1, peer, recv2).wait_send()

    def drain(s, carry):
        for piece in range(PIECES):
            hop(s, piece).wait_send()
        return carry

    lax.fori_loop(0, last - 1, drain, 0)
    for piece in range(PIECES):
        hop(last - 1, piece).wait_recv()
        out_ref[:, piece * width : (piece + 1) * width] = (ring[last, piece] + held[piece]).astype(BF16)

    for piece in range(PIECES):
        hop(last - 1, piece).wait_send()


def solution(mesh):
    n_ctx, n_head = mesh.shape["ctx"], mesh.shape["head"]

    def body(features, gate_values, write_proj, read_proj, step_size, log_decay, starts, skip_weight, norm_gain, out_weight):
        tokens, chans = features.shape
        heads = step_size.shape[0]
        blocks = tokens // SPAN
        width_out = out_weight.shape[1]
        chunk = tokens // n_head
        half = chans // 2
        chips = n_ctx // 2
        across = half // 128
        deep = NSTATE // (chips // across)
        width = width_out // PIECES
        dma = pltpu.SemaphoreType.DMA
        scratch = [
            pltpu.VMEM((blocks, SPAN, chans), BF16),
            pltpu.VMEM((blocks, SPAN, chans), BF16),
            pltpu.VMEM((blocks, SPAN, NSTATE), BF16),
            pltpu.VMEM((blocks, SPAN, NSTATE), BF16),
            pltpu.VMEM((heads, tokens), F32),
            pltpu.VMEM((heads, tokens), F32),
            pltpu.VMEM((1, tokens), jnp.int32),
            pltpu.VMEM((1, heads), F32),
            pltpu.VMEM((1, chans), F32),
            pltpu.VMEM((chans, width_out), BF16),
            pltpu.VMEM((blocks, NSTATE, SPAN), BF16),
            pltpu.VMEM((blocks, heads, SPAN), F32),
            pltpu.VMEM((blocks, 8, SPAN), F32),
            pltpu.VMEM((tokens, NSTATE), F32),
            pltpu.VMEM((NSTATE, chans), BF16),
            pltpu.VMEM((1, chans), F32),
            pltpu.VMEM((n_head, chunk, chans), F32),
            pltpu.VMEM((n_head, chunk, chans), F32),
            pltpu.VMEM((2, NSTATE, half), F32),
            pltpu.VMEM((2, 8, half), F32),
            pltpu.VMEM((2, NSTATE + 8, half), F32),
            pltpu.VMEM((NSTATE + 8, half), F32),
            pltpu.VMEM((NSTATE + 8, half), F32),
            pltpu.VMEM((chips, deep + 1, 128), F32),
            pltpu.VMEM((chips, deep + 1, 128), F32),
            pltpu.VMEM((chips, deep, 128), F32),
            pltpu.VMEM((chips, deep, 128), F32),
            pltpu.VMEM((NSTATE, half), F32),
            pltpu.VMEM((NSTATE, half), F32),
            pltpu.VMEM((blocks, 2, NSTATE, half), BF16),
            pltpu.VMEM((chunk, chans), BF16),
            pltpu.VMEM((n_head, PIECES, chunk, width), F32),
            pltpu.VMEM((PIECES, chunk, width), F32),
            dma((10,)),
            dma((2,)),
            dma((2,)),
            dma((2, chips)),
            dma((2, chips)),
            dma((n_head - 1, PIECES)),
            dma((n_head - 1, PIECES)),
        ]
        return pl.pallas_call(
            functools.partial(kernel, n_ctx, n_head),
            out_shape=jax.ShapeDtypeStruct((chunk, width_out), BF16),
            in_specs=[pl.BlockSpec(memory_space=pltpu.HBM)] * 10,
            out_specs=pl.BlockSpec(memory_space=pltpu.VMEM),
            scratch_shapes=scratch,
            compiler_params=pltpu.CompilerParams(
                collective_id=0, has_side_effects=True, vmem_limit_bytes=48 * 1024 * 1024
            ),
        )(
            *(
                pltpu.with_memory_space_constraint(value, pltpu.HBM)
                for value in (
                    features.reshape(blocks, SPAN, chans),
                    gate_values.reshape(blocks, SPAN, chans),
                    write_proj.reshape(blocks, SPAN, NSTATE),
                    read_proj.reshape(blocks, SPAN, NSTATE),
                    step_size,
                    log_decay,
                    starts.reshape(1, tokens),
                    skip_weight.reshape(1, heads),
                    norm_gain.reshape(1, chans),
                    out_weight,
                )
            )
        )

    placed = (
        P("ctx", "head"),
        P("ctx", "head"),
        P("ctx", "head"),
        P("ctx", "head"),
        P("head", "ctx"),
        P("head", "ctx"),
        P("ctx"),
        P("head"),
        P("head"),
        P("head", None),
    )
    return jax.shard_map(
        body, mesh=mesh, in_specs=placed, out_specs=P(("ctx", "head"), None), check_vma=False
    )
```
